32 devices in a mesh: patch: 8 (over z, x), feat: 4 (over y, core).
Axes of the slice: x: 2, y: 2, z: 4, core: 2. Of those that a mesh axis runs over, the one named last changes fastest.
Arguments:
- nodes: bfloat16 [5120, 512], P(('patch', 'feat')), may hold values from -6 to 6
- edges: bfloat16 [40960, 512], P(('patch', 'feat')), may hold values from -6 to 6
- receivers: int32 [40960], P(('patch', 'feat')), may hold values from 0 to 639
- sender_slot: int32 [40960], P(('patch', 'feat')), may hold values from 0 to 831
- send_rows: int32 [8, 4, 8, 24], P('patch', 'feat'), may hold values from 0 to 159
- live_edges: int32 [32], P(('patch', 'feat')), may hold values from 1 to 1280, 30720 in all
- edge_w1: bfloat16 [1536, 512], replicated, may hold values from -0.15625 to 0.15625
- edge_b1: float32 [512], replicated, may hold values from -3 to 3
- edge_w2: bfloat16 [512, 512], replicated, may hold values from -0.25 to 0.25
- edge_gain: float32 [512], replicated, may hold values from 0.5 to 1.5
- node_w1: bfloat16 [1024, 512], replicated, may hold values from -0.1875 to 0.1875
- node_b1: float32 [512], replicated, may hold values from -3 to 3
- node_w2: bfloat16 [512, 512], replicated, may hold values from -0.25 to 0.25
- node_gain: float32 [512], replicated, may hold values from 0.5 to 1.5
Outputs:
- edges_out: bfloat16 [40960, 512], P(('patch', 'feat'))
- nodes_out: bfloat16 [5120, 512], P(('patch', 'feat'))
The draws below stay inside these ranges and needn't reach their ends.
Inputs may be any that keep to these rules, and one draw needn't show every extreme that they name: `live_edges`: edge slots at or past a device's count are padding.
All inputs are finite; a program needn't handle non-finite values.
Results may differ from the reference program's by a relative error of at most 0.0052.
Values may be sent and summed in bfloat16 or wider, within the bound.
A program may use at most 64 MiB of HBM per device.

```python
import math
import jax
import jax.numpy as jnp
import numpy as np
from jax import lax

D = 512
NODE_SUB = 160
EDGE_DEV = 1280
CAP = 24
NODE_DEV = 640
NODES = 5120
EDGES = 40960
N_PATCH = 8
N_FEAT = 4
DEVICES = 32


def plant(array, own_key, least, high):
    dims = array.shape
    index_at = [jax.random.randint(jax.random.fold_in(own_key, axis), (), 0, dims[axis]) for axis in range(len(dims))]
    array = array.at[tuple(index_at)].set(least)
    longest = dims.index(max(dims))
    index_at[longest] = (index_at[longest] + 1) % dims[longest]
    return array.at[tuple(index_at)].set(high)


def block_levels(rng, shape, shards, smallest, high):
    gain, own = 1.0, jax.random.fold_in(rng, 6)
    for position, shards_of in shards:
        heights = jnp.exp(jax.random.uniform(jax.random.fold_in(own, position), (shards_of,), jnp.float32, smallest / len(shards), high / len(shards)))
        gain = gain * jnp.repeat(heights, shape[position] // shards_of).reshape([-1 if axis == position else 1 for axis in range(len(shape))])
    return gain


def profile(number_of, total, most, lean):
    weights = [(1 << 20) // math.isqrt(grade ** lean) + 1 for grade in range(2, number_of + 1)]
    rest, holding = total - most - (number_of - 1), [1] * (number_of - 1)
    while rest > 0:
        candidates = [i for i in range(number_of - 1) if holding[i] < most]
        mass, budget = sum([weights[i] for i in candidates]), rest
        for i in candidates:
            more = min(most - holding[i], max(1, budget * weights[i] // mass), rest)
            holding[i] = holding[i] + more
            rest = rest - more
    return np.array([most] + holding)


def uneven_parts(rng, amount, total, most, slope):
    if amount == 2:
        one = jax.random.randint(rng, (), max(1, total - most), min(most, total - 1) + 1)
        return jnp.stack([one, total - one])
    sizes = jnp.asarray(profile(amount, total, most, slope), jnp.int32)
    pairs = (amount - 1) // 2
    donor, receiver = sizes[1:1 + 2 * pairs:2], sizes[2:2 + 2 * pairs:2]
    slack = jnp.minimum(donor - 1, most - receiver)
    moved = jax.random.randint(jax.random.fold_in(rng, 1), (pairs,), 0, 1 << 20) % (slack + 1)
    sizes = sizes.at[1:1 + 2 * pairs:2].set(donor - moved).at[2:2 + 2 * pairs:2].set(receiver + moved)
    return sizes[jax.random.permutation(jax.random.fold_in(rng, 2), amount)]


def scatter_about(key, extent, scale, reach, cuts=(), held_as=jnp.bfloat16):
    values = scale * jax.random.normal(key, extent, jnp.float32)
    if cuts:
        values = values * block_levels(key, extent, cuts, -0.22, 0.18)
    return jnp.clip(values, -reach, reach).astype(held_as)


def setup_inputs(seed: int = 0) -> dict:
    arg_keys = jax.random.split(jax.random.key(seed), 15)
    nodes = scatter_about(arg_keys[0], (NODES, D), 1.0, 6.0, ((0, 32),))
    edges = scatter_about(arg_keys[1], (EDGES, D), 1.0, 6.0, ((0, 32),))
    receivers = plant(jax.random.randint(arg_keys[2], (EDGES,), 0, NODE_DEV), jax.random.fold_in(arg_keys[2], 1), 0, NODE_DEV - 1).astype(jnp.int32)
    sender_slot = plant(jax.random.randint(arg_keys[3], (EDGES,), 0, NODE_DEV + N_PATCH * CAP), jax.random.fold_in(arg_keys[3], 1), 0, (NODE_DEV + N_PATCH * CAP) - 1).astype(jnp.int32)
    send_rows = plant(jax.random.randint(arg_keys[4], (N_PATCH, N_FEAT, N_PATCH, CAP), 0, NODE_SUB), jax.random.fold_in(arg_keys[4], 1), 0, NODE_SUB - 1).astype(jnp.int32)
    live_edges = uneven_parts(arg_keys[5], DEVICES, DEVICES * EDGE_DEV * 3 // 4, EDGE_DEV, 1).astype(jnp.int32)
    edge_w1 = scatter_about(arg_keys[6], (3 * D, D), (3 * D) ** -0.5, 0.15625)
    edge_b1 = scatter_about(arg_keys[7], (D,), 0.5, 3.0, (), jnp.float32)
    edge_w2 = scatter_about(arg_keys[8], (D, D), D ** -0.5, 0.25)
    edge_gain = jnp.clip(1.0 + 0.1 * jax.random.normal(arg_keys[9], (D,), jnp.float32), 0.5, 1.5)
    node_w1 = scatter_about(arg_keys[10], (2 * D, D), (2 * D) ** -0.5, 0.1875)
    node_b1 = scatter_about(arg_keys[11], (D,), 0.5, 3.0, (), jnp.float32)
    node_w2 = scatter_about(arg_keys[12], (D, D), D ** -0.5, 0.25)
    node_gain = jnp.clip(1.0 + 0.1 * jax.random.normal(arg_keys[13], (D,), jnp.float32), 0.5, 1.5)
    return dict(nodes=nodes, edges=edges, receivers=receivers, sender_slot=sender_slot, send_rows=send_rows, live_edges=live_edges, edge_w1=edge_w1, edge_b1=edge_b1, edge_w2=edge_w2, edge_gain=edge_gain, node_w1=node_w1, node_b1=node_b1, node_w2=node_w2, node_gain=node_gain)


epsilon = 1e-05

def layer_norm(values, scales):
    average = lax.optimization_barrier(jnp.mean(values, axis=-1, keepdims=True))
    centred = values - average
    variance = lax.optimization_barrier(jnp.mean(centred * centred, axis=-1, keepdims=True))
    return centred * lax.rsqrt(variance + epsilon) * scales

def edge_change(edge_rows, sender_feat, receiver_feat, edge_w1, edge_b1, edge_w2, edge_gain):
    latent = edge_rows.shape[1]
    first = jnp.dot(edge_rows, edge_w1[:latent], preferred_element_type=jnp.float32)
    first = first + jnp.dot(sender_feat, edge_w1[latent:2 * latent], preferred_element_type=jnp.float32)
    first = first + jnp.dot(receiver_feat, edge_w1[2 * latent:], preferred_element_type=jnp.float32)
    hidden = jax.nn.silu(first + edge_b1).astype(jnp.bfloat16)
    return layer_norm(jnp.dot(hidden, edge_w2, preferred_element_type=jnp.float32), edge_gain)

def node_change(node_rows, incoming, node_w1, node_b1, node_w2, node_gain):
    latent = node_rows.shape[1]
    first = jnp.dot(node_rows, node_w1[:latent], preferred_element_type=jnp.float32)
    first = first + jnp.dot(incoming, node_w1[latent:], preferred_element_type=jnp.float32)
    hidden = jax.nn.silu(first + node_b1).astype(jnp.bfloat16)
    return layer_norm(jnp.dot(hidden, node_w2, preferred_element_type=jnp.float32), node_gain)

def reference(nodes, edges, receivers, sender_slot, send_rows, live_edges, edge_w1, edge_b1, edge_w2, edge_gain, node_w1, node_b1, node_w2, node_gain):
    groups = N_PATCH * N_FEAT
    edge_ids = jnp.arange(groups * EDGE_DEV, dtype=jnp.int32)
    device_index = edge_ids // EDGE_DEV
    patch_index = device_index // N_FEAT
    feat_index = device_index % N_FEAT
    is_local = sender_slot < NODE_DEV
    remote_slot = jnp.maximum(sender_slot - NODE_DEV, 0)
    source_patch = remote_slot // CAP
    slot_column = remote_slot % CAP
    listed_row = send_rows[source_patch, feat_index, patch_index, slot_column]
    senders = jnp.where(is_local, patch_index * NODE_DEV + sender_slot, source_patch * NODE_DEV + feat_index * NODE_SUB + listed_row).astype(jnp.int32)
    receiver_rows = (patch_index * NODE_DEV + receivers).astype(jnp.int32)
    alive = edge_ids % EDGE_DEV < live_edges[device_index]
    latent = edges.shape[1]

    def per_device(packs):
        edge_rows, sender_ids, receiver_ids, alive_rows = packs
        change = edge_change(edge_rows, jnp.take(nodes, sender_ids, axis=0), jnp.take(nodes, receiver_ids, axis=0), edge_w1, edge_b1, edge_w2, edge_gain)
        return (edge_rows.astype(jnp.float32) + jnp.where(alive_rows[:, None], change, 0.0)).astype(jnp.bfloat16)
    edges_out = lax.map(per_device, (edges.reshape(groups, EDGE_DEV, latent), senders.reshape(groups, EDGE_DEV), receiver_rows.reshape(groups, EDGE_DEV), alive.reshape(groups, EDGE_DEV)))
    edges_out = edges_out.reshape(groups * EDGE_DEV, latent)
    summed = jax.ops.segment_sum(jnp.where(alive[:, None], edges_out.astype(jnp.float32), 0.0), receiver_rows, num_segments=NODES)
    incoming = summed.astype(jnp.bfloat16)
    change = node_change(nodes, incoming, node_w1, node_b1, node_w2, node_gain)
    nodes_out = (nodes.astype(jnp.float32) + change).astype(jnp.bfloat16)
    return (edges_out, nodes_out)
```

```python
import functools

import jax
import jax.numpy as jnp
from jax import lax
from jax.experimental import pallas as pl
from jax.experimental.pallas import tpu as pltpu
from jax.sharding import PartitionSpec as P

epsilon = 1e-05
MESH = pl.DeviceIdType.MESH
LANES = 128
F32, BF16 = jnp.float32, jnp.bfloat16


def dot(a, b):
    return jnp.dot(a, b, preferred_element_type=F32)


def layer_norm(values, scales):
    average = jnp.mean(values, axis=-1, keepdims=True)
    centred = values - average
    variance = jnp.mean(centred * centred, axis=-1, keepdims=True)
    return centred * lax.rsqrt(variance + epsilon) * scales


def column(row):
    parts = []
    for at in range(0, row.shape[1], LANES):
        block = jnp.broadcast_to(row[:, at : at + LANES], (LANES, LANES))
        parts.append(block.T[:, :1])
    return jnp.concatenate(parts, axis=0)


def mask(hit):
    return jnp.where(hit, 1.0, 0.0).astype(BF16)


def low_bit(number):
    return number & -number


def kernel(
    n_patch,
    n_feat,
    cap,
    tile,
    live_ref,
    nodes_ref,
    recv_ref,
    slot_ref,
    list_ref,
    b1_ref,
    gain_ref,
    nb1_ref,
    ngain_ref,
    edges_hbm,
    w1_hbm,
    w2_hbm,
    nw1_hbm,
    nw2_hbm,
    edges_out,
    nodes_out,
    edges_v,
    w1,
    w2,
    nw1,
    nw2,
    packed,
    remote,
    patch,
    table,
    first,
    out_v,
    send_v,
    got_v,
    load_sem,
    store_sem,
    list_send,
    list_recv,
    node_send,
    node_recv,
    sum_send,
    sum_recv,
):
    me_p, me_f = lax.axis_index("patch"), lax.axis_index("feat")
    own, latent = nodes_ref.shape
    count = edges_v.shape[0]
    slots = packed.shape[1]
    n_local = n_feat * own
    n_table = n_local + n_patch * slots
    bits = [1 << i for i in range(n_feat.bit_length() - 1)]

    def feat_peer(bit):
        return jnp.bitwise_xor(me_f, bit)

    def patch_peer(step):
        return lax.rem(me_p + step, n_patch)

    barrier = pltpu.get_barrier_semaphore()
    for bit in bits:
        pl.semaphore_signal(
            barrier, inc=1, device_id=(me_p, feat_peer(bit)), device_id_type=MESH
        )
    for step in range(1, n_patch):
        pl.semaphore_signal(
            barrier, inc=1, device_id=(patch_peer(step), me_f), device_id_type=MESH
        )

    loads = []
    for i, (src, dst) in enumerate(
        ((w1_hbm, w1), (edges_hbm, edges_v), (w2_hbm, w2), (nw1_hbm, nw1), (nw2_hbm, nw2))
    ):
        loads.append(pltpu.make_async_copy(src, dst, load_sem.at[i]))
        loads[-1].start()

    wanted = column(list_ref[...])
    rows = wanted.shape[0]
    pick = mask(wanted == lax.broadcasted_iota(jnp.int32, (rows, own), 1))
    packed[...] = dot(pick, nodes_ref[...])[: n_patch * slots].astype(BF16).reshape(packed.shape)
    patch[me_f] = nodes_ref[...]

    pl.semaphore_wait(barrier, len(bits) + n_patch - 1)

    def node_copy(have, bit):
        to = have | bit
        block = jnp.bitwise_xor(me_f, have)
        return pltpu.make_async_remote_copy(
            src_ref=nodes_ref if have == 0 else patch.at[block],
            dst_ref=patch.at[block],
            send_sem=node_send.at[to],
            recv_sem=node_recv.at[to],
            device_id=(me_p, feat_peer(bit)),
            device_id_type=MESH,
        )

    node_copies = {}
    for bit in reversed(bits):
        node_copies[bit] = node_copy(0, bit)
        node_copies[bit].start()
    list_copies = []
    for step in range(1, n_patch):
        to = patch_peer(step)
        copy = pltpu.make_async_remote_copy(
            src_ref=packed.at[to],
            dst_ref=remote.at[me_p],
            send_sem=list_send.at[step],
            recv_sem=list_recv.at[step],
            device_id=(to, me_f),
            device_id_type=MESH,
        )
        copy.start()
        list_copies.append(copy)
    remote[me_p] = packed[me_p]

    loads[0].wait()
    loads[1].wait()

    def first_part(at):
        span = pl.ds(pl.multiple_of(at * tile, tile), tile)
        first[span, :] = dot(edges_v[span, :], w1[:latent, :]) + b1_ref[...]

    halfway = (count // tile) // 2
    pl.loop(0, halfway)(first_part)

    for have in range(1, n_feat):
        if low_bit(have) > 1:
            node_copies[have].wait_recv()
            for bit in reversed([b for b in bits if b < low_bit(have)]):
                node_copies[have | bit] = node_copy(have, bit)
                node_copies[have | bit].start()

    pl.loop(halfway, count // tile)(first_part)

    for have in range(1, n_feat):
        if low_bit(have) == 1:
            node_copies[have].wait_recv()
    gathered = patch[...].reshape(n_local, latent)
    table[:n_local, :] = dot(gathered, w1[latent : 2 * latent, :]).astype(BF16)
    table[n_table:, :] = dot(gathered, w1[2 * latent :, :]).astype(BF16)
    for copy in list_copies:
        copy.wait_recv()
    listed = remote[...].reshape(n_patch * slots, latent)
    table[n_local:n_table, :] = dot(listed, w1[latent : 2 * latent, :]).astype(BF16)

    live = live_ref[0]
    loads[2].wait()

    def store(at):
        span = pl.ds(pl.multiple_of(at * tile, tile), tile)
        return pltpu.make_async_copy(out_v.at[span, :], edges_out.at[span, :], store_sem.at[at])

    def edge_part(at):
        span = pl.ds(pl.multiple_of(at * tile, tile), tile)
        receiver = column(recv_ref[:, span])
        slot = slot_ref[:, span]
        beyond = slot - n_local
        source = ((beyond.astype(F32) + 0.5) * (1.0 / cap)).astype(jnp.int32)
        slot = jnp.where(beyond < 0, slot, slot + source * (slots - cap))
        sender = column(slot)
        hits = jnp.concatenate(
            [
                mask(sender == lax.broadcasted_iota(jnp.int32, (tile, n_table), 1)),
                mask(receiver == lax.broadcasted_iota(jnp.int32, (tile, n_local), 1)),
            ],
            axis=1,
        )
        hidden = jax.nn.silu(first[span, :] + dot(hits, table[...])).astype(BF16)
        change = layer_norm(dot(hidden, w2[...]), gain_ref[...])
        place = lax.broadcasted_iota(jnp.int32, (tile, latent), 0) + at * tile
        change = jnp.where(place < live, change, 0.0)
        out_v[span, :] = (edges_v[span, :].astype(F32) + change).astype(BF16)
        store(at).start()

    pl.loop(0, count // tile)(edge_part)

    live_recv = jnp.where(
        lax.broadcasted_iota(jnp.int32, (1, count), 1) < live, recv_ref[...], -1
    )

    sum_copies = {}
    total = None
    for have in sorted(range(n_feat), key=lambda d: (low_bit(d) or n_feat, -d)):
        block = jnp.bitwise_xor(me_f, have)
        ids = lax.broadcasted_iota(jnp.int32, (own, count), 0) + block * own
        total = dot(mask(ids == live_recv), out_v[...])
        if have == 0:
            loads[3].wait()
            own_first = dot(nodes_ref[...], nw1[:latent, :]) + nb1_ref[...]
            loads[4].wait()
        for bit in bits:
            if have == 0 or bit < low_bit(have):
                sum_copies[have | bit].wait_recv()
                total = total + got_v[have | bit].astype(F32)
        if have:
            send_v[have] = total.astype(BF16)
            sum_copies[have] = pltpu.make_async_remote_copy(
                src_ref=send_v.at[have],
                dst_ref=got_v.at[have],
                send_sem=sum_send.at[have],
                recv_sem=sum_recv.at[have],
                device_id=(me_p, feat_peer(low_bit(have))),
                device_id_type=MESH,
            )
            sum_copies[have].start()

    hidden = jax.nn.silu(own_first + dot(total.astype(BF16), nw1[latent:, :])).astype(BF16)
    change = layer_norm(dot(hidden, nw2[...]), ngain_ref[...])
    nodes_out[...] = (nodes_ref[...].astype(F32) + change).astype(BF16)

    for copy in list(node_copies.values()) + list_copies + list(sum_copies.values()):
        copy.wait_send()
    for at in range(count // tile):
        store(at).wait()


def local(n_patch, n_feat, *args):
    (nodes, edges, receivers, sender_slot, send_rows, live_edges) = args[:6]
    (edge_w1, edge_b1, edge_w2, edge_gain, node_w1, node_b1, node_w2, node_gain) = args[6:]
    own, latent = nodes.shape
    count = edges.shape[0]
    cap = send_rows.shape[3]
    slots = -(-cap // 16) * 16
    while (n_feat * own + n_patch * slots) % LANES:
        slots += 16
    tile = next(t for t in (256, 128) if count % t == 0)
    listed = jnp.pad(send_rows[0, 0], ((0, 0), (0, slots - cap)), constant_values=-1)
    listed = listed.reshape(1, -1)
    listed = jnp.pad(listed, ((0, 0), (0, -listed.shape[1] % LANES)), constant_values=-1)
    n_table = n_feat * own + n_patch * slots
    vmem = pl.BlockSpec(memory_space=pltpu.VMEM)
    hbm = pl.BlockSpec(memory_space=pl.ANY)
    dma = pltpu.SemaphoreType.DMA
    return pl.pallas_call(
        functools.partial(kernel, n_patch, n_feat, cap, tile),
        out_shape=(
            jax.ShapeDtypeStruct(edges.shape, BF16),
            jax.ShapeDtypeStruct(nodes.shape, BF16),
        ),
        in_specs=[pl.BlockSpec(memory_space=pltpu.SMEM)] + [vmem] * 8 + [hbm] * 5,
        out_specs=(hbm, vmem),
        scratch_shapes=[
            pltpu.VMEM(edges.shape, BF16),
            pltpu.VMEM(edge_w1.shape, BF16),
            pltpu.VMEM(edge_w2.shape, BF16),
            pltpu.VMEM(node_w1.shape, BF16),
            pltpu.VMEM(node_w2.shape, BF16),
            pltpu.VMEM((n_patch, slots, latent), BF16),
            pltpu.VMEM((n_patch, slots, latent), BF16),
            pltpu.VMEM((n_feat, own, latent), BF16),
            pltpu.VMEM((n_table + n_feat * own, latent), BF16),
            pltpu.VMEM(edges.shape, F32),
            pltpu.VMEM(edges.shape, BF16),
            pltpu.VMEM((n_feat, own, latent), BF16),
            pltpu.VMEM((n_feat, own, latent), BF16),
            dma((5,)),
            dma((count // tile,)),
            dma((n_patch,)),
            dma((n_patch,)),
            dma((n_feat,)),
            dma((n_feat,)),
            dma((n_feat,)),
            dma((n_feat,)),
        ],
        compiler_params=pltpu.CompilerParams(
            collective_id=0, has_side_effects=True, vmem_limit_bytes=60 * 1024 * 1024
        ),
    )(
        live_edges,
        nodes,
        receivers.reshape(1, -1),
        sender_slot.reshape(1, -1),
        listed,
        edge_b1.reshape(1, -1),
        edge_gain.reshape(1, -1),
        node_b1.reshape(1, -1),
        node_gain.reshape(1, -1),
        edges,
        edge_w1,
        edge_w2,
        node_w1,
        node_w2,
    )


def solution(mesh):
    both = P(("patch", "feat"))
    rows = P(("patch", "feat"), None)
    placed = (rows, rows, both, both, P("patch", "feat", None, None), both) + (P(),) * 8
    return jax.shard_map(
        functools.partial(local, mesh.shape["patch"], mesh.shape["feat"]),
        mesh=mesh,
        in_specs=placed,
        out_specs=(rows, rows),
        check_vma=False,
    )
```

```python
import functools

import jax
import jax.numpy as jnp
from jax import lax
from jax.experimental import pallas as pl
from jax.experimental.pallas import tpu as pltpu
from jax.sharding import PartitionSpec as P

epsilon = 1e-05
MESH = pl.DeviceIdType.MESH
LANES = 128
F32, BF16 = jnp.float32, jnp.bfloat16


def dot(a, b):
    return jnp.dot(a, b, preferred_element_type=F32)


def layer_norm(values, scales):
    average = jnp.mean(values, axis=-1, keepdims=True)
    centred = values - average
    variance = jnp.mean(centred * centred, axis=-1, keepdims=True)
    return centred * lax.rsqrt(variance + epsilon) * scales


def column(rows):
    parts = [jnp.broadcast_to(row, (LANES, LANES)).T[:, :1] for row in rows]
    return jnp.concatenate(parts, axis=0)


def mask(hit):
    return jnp.where(hit, 1.0, 0.0).astype(BF16)


def low_bit(number):
    return number & -number


def kernel(
    n_patch,
    n_feat,
    cap,
    tile,
    live_ref,
    nodes_ref,
    recv_ref,
    slot_ref,
    list_ref,
    b1_ref,
    gain_ref,
    nb1_ref,
    ngain_ref,
    edges_hbm,
    w1_hbm,
    w2_hbm,
    nw1_hbm,
    nw2_hbm,
    edges_out,
    nodes_out,
    edges_v,
    w1,
    w2,
    nw1,
    nw2,
    packed,
    remote,
    patch,
    table,
    first,
    hits,
    grid_v,
    out_v,
    send_v,
    got_v,
    load_sem,
    store_sem,
    list_send,
    list_recv,
    node_send,
    node_recv,
    sum_send,
    sum_recv,
):
    me_p, me_f = lax.axis_index("patch"), lax.axis_index("feat")
    own, latent = nodes_ref.shape
    count = edges_v.shape[0]
    slots = packed.shape[1]
    n_local = n_feat * own
    n_table = n_local + n_patch * slots
    bits = [1 << i for i in range(n_feat.bit_length() - 1)]

    def feat_peer(bit):
        return jnp.bitwise_xor(me_f, bit)

    def patch_peer(step):
        return lax.rem(me_p + step, n_patch)

    barrier = pltpu.get_barrier_semaphore()
    for bit in bits:
        pl.semaphore_signal(
            barrier, inc=1, device_id=(me_p, feat_peer(bit)), device_id_type=MESH
        )
    for step in range(1, n_patch):
        pl.semaphore_signal(
            barrier, inc=1, device_id=(patch_peer(step), me_f), device_id_type=MESH
        )

    loads = []
    for i, (src, dst) in enumerate(
        ((w1_hbm, w1), (edges_hbm, edges_v), (w2_hbm, w2), (nw1_hbm, nw1), (nw2_hbm, nw2))
    ):
        loads.append(pltpu.make_async_copy(src, dst, load_sem.at[i]))
        loads[-1].start()

    pl.semaphore_wait(barrier, len(bits) + n_patch - 1)

    def node_copy(have, bit):
        to = have | bit
        block = jnp.bitwise_xor(me_f, have)
        return pltpu.make_async_remote_copy(
            src_ref=nodes_ref if have == 0 else patch.at[block],
            dst_ref=patch.at[block],
            send_sem=node_send.at[to],
            recv_sem=node_recv.at[to],
            device_id=(me_p, feat_peer(bit)),
            device_id_type=MESH,
        )

    node_copies = {}
    for bit in reversed(bits):
        node_copies[bit] = node_copy(0, bit)
        node_copies[bit].start()
    grid_v[...] = jnp.full(grid_v.shape, -1, jnp.int32)
    grid_v[:n_patch, :cap] = list_ref[...]
    lists = grid_v[...].T
    wanted = jnp.concatenate([lists[:slots, p : p + 1] for p in range(n_patch)], axis=0)
    pick = mask(wanted == lax.broadcasted_iota(jnp.int32, (n_patch * slots, own), 1))
    packed[...] = dot(pick, nodes_ref[...]).astype(BF16).reshape(packed.shape)
    patch[me_f] = nodes_ref[...]

    per_tile = tile // LANES

    def hit_part(at):
        span = pl.ds(pl.multiple_of(at * tile, tile), tile)
        lines = [pl.ds(at * per_tile + i, 1) for i in range(per_tile)]
        receiver = column([recv_ref[line, :] for line in lines])
        senders = []
        for line in lines:
            slot = slot_ref[line, :]
            beyond = slot - n_local
            source = ((beyond.astype(F32) + 0.5) * (1.0 / cap)).astype(jnp.int32)
            senders.append(jnp.where(beyond < 0, slot, slot + source * (slots - cap)))
        sender = column(senders)
        hits[span, :n_table] = mask(
            sender == lax.broadcasted_iota(jnp.int32, (tile, n_table), 1)
        )
        hits[span, n_table:] = mask(
            receiver == lax.broadcasted_iota(jnp.int32, (tile, n_local), 1)
        )

    halfway = (count // tile) // 2
    pl.loop(0, halfway)(hit_part)

    list_copies = []
    for step in range(1, n_patch):
        to = patch_peer(step)
        copy = pltpu.make_async_remote_copy(
            src_ref=packed.at[to],
            dst_ref=remote.at[me_p],
            send_sem=list_send.at[step],
            recv_sem=list_recv.at[step],
            device_id=(to, me_f),
            device_id_type=MESH,
        )
        copy.start()
        list_copies.append(copy)
    remote[me_p] = packed[me_p]

    loads[0].wait()
    loads[1].wait()

    def first_part(at):
        span = pl.ds(pl.multiple_of(at * tile, tile), tile)
        first[span, :] = dot(edges_v[span, :], w1[:latent, :]) + b1_ref[...]

    pl.loop(0, count // tile)(first_part)

    for have in range(1, n_feat):
        if low_bit(have) > 1:
            node_copies[have].wait_recv()
            for bit in reversed([b for b in bits if b < low_bit(have)]):
                node_copies[have | bit] = node_copy(have, bit)
                node_copies[have | bit].start()

    pl.loop(halfway, count // tile)(hit_part)

    for have in range(1, n_feat):
        if low_bit(have) == 1:
            node_copies[have].wait_recv()
    gathered = patch[...].reshape(n_local, latent)
    table[:n_local, :] = dot(gathered, w1[latent : 2 * latent, :]).astype(BF16)
    table[n_table:, :] = dot(gathered, w1[2 * latent :, :]).astype(BF16)
    for copy in list_copies:
        copy.wait_recv()
    listed = remote[...].reshape(n_patch * slots, latent)
    table[n_local:n_table, :] = dot(listed, w1[latent : 2 * latent, :]).astype(BF16)

    live = live_ref[0]
    loads[2].wait()

    def store(at):
        span = pl.ds(pl.multiple_of(at * tile, tile), tile)
        return pltpu.make_async_copy(out_v.at[span, :], edges_out.at[span, :], store_sem.at[at])

    def edge_part(at):
        span = pl.ds(pl.multiple_of(at * tile, tile), tile)
        hidden = jax.nn.silu(first[span, :] + dot(hits[span, :], table[...])).astype(BF16)
        change = layer_norm(dot(hidden, w2[...]), gain_ref[...])
        place = lax.broadcasted_iota(jnp.int32, (tile, latent), 0) + at * tile
        change = jnp.where(place < live, change, 0.0)
        out_v[span, :] = (edges_v[span, :].astype(F32) + change).astype(BF16)
        store(at).start()

    pl.loop(0, count // tile)(edge_part)

    live_recv = []
    for line in range(count // LANES):
        place = lax.broadcasted_iota(jnp.int32, (1, LANES), 1) + line * LANES
        live_recv.append(jnp.where(place < live, recv_ref[line : line + 1, :], -1))

    sum_copies = {}
    total = None
    for have in sorted(range(n_feat), key=lambda d: (low_bit(d) or n_feat, -d)):
        block = jnp.bitwise_xor(me_f, have)
        ids = lax.broadcasted_iota(jnp.int32, (own, LANES), 0) + block * own
        spread = jnp.concatenate([mask(ids == line) for line in live_recv], axis=1)
        total = dot(spread, out_v[...])
        if have == 0:
            loads[3].wait()
            own_first = dot(nodes_ref[...], nw1[:latent, :]) + nb1_ref[...]
            loads[4].wait()
        for bit in bits:
            if have == 0 or bit < low_bit(have):
                sum_copies[have | bit].wait_recv()
                total = total + got_v[have | bit].astype(F32)
        if have:
            send_v[have] = total.astype(BF16)
            sum_copies[have] = pltpu.make_async_remote_copy(
                src_ref=send_v.at[have],
                dst_ref=got_v.at[have],
                send_sem=sum_send.at[have],
                recv_sem=sum_recv.at[have],
                device_id=(me_p, feat_peer(low_bit(have))),
                device_id_type=MESH,
            )
            sum_copies[have].start()

    hidden = jax.nn.silu(own_first + dot(total.astype(BF16), nw1[latent:, :])).astype(BF16)
    change = layer_norm(dot(hidden, nw2[...]), ngain_ref[...])
    nodes_out[...] = (nodes_ref[...].astype(F32) + change).astype(BF16)

    for copy in list(node_copies.values()) + list_copies + list(sum_copies.values()):
        copy.wait_send()
    for at in range(count // tile):
        store(at).wait()


def local(n_patch, n_feat, *args):
    (nodes, edges, receivers, sender_slot, send_rows, live_edges) = args[:6]
    (edge_w1, edge_b1, edge_w2, edge_gain, node_w1, node_b1, node_w2, node_gain) = args[6:]
    own, latent = nodes.shape
    count = edges.shape[0]
    cap = send_rows.shape[3]
    slots = -(-cap // 16) * 16
    while (n_feat * own + n_patch * slots) % LANES:
        slots += 16
    tile = next(t for t in (256, 128) if count % t == 0)
    n_table = n_feat * own + n_patch * slots
    vmem = pl.BlockSpec(memory_space=pltpu.VMEM)
    hbm = pl.BlockSpec(memory_space=pl.ANY)
    dma = pltpu.SemaphoreType.DMA
    return pl.pallas_call(
        functools.partial(kernel, n_patch, n_feat, cap, tile),
        out_shape=(
            jax.ShapeDtypeStruct(edges.shape, BF16),
            jax.ShapeDtypeStruct(nodes.shape, BF16),
        ),
        in_specs=[pl.BlockSpec(memory_space=pltpu.SMEM)] + [vmem] * 8 + [hbm] * 5,
        out_specs=(hbm, vmem),
        scratch_shapes=[
            pltpu.VMEM(edges.shape, BF16),
            pltpu.VMEM(edge_w1.shape, BF16),
            pltpu.VMEM(edge_w2.shape, BF16),
            pltpu.VMEM(node_w1.shape, BF16),
            pltpu.VMEM(node_w2.shape, BF16),
            pltpu.VMEM((n_patch, slots, latent), BF16),
            pltpu.VMEM((n_patch, slots, latent), BF16),
            pltpu.VMEM((n_feat, own, latent), BF16),
            pltpu.VMEM((n_table + n_feat * own, latent), BF16),
            pltpu.VMEM(edges.shape, F32),
            pltpu.VMEM((count, n_table + n_feat * own), BF16),
            pltpu.VMEM((LANES, LANES), jnp.int32),
            pltpu.VMEM(edges.shape, BF16),
            pltpu.VMEM((n_feat, own, latent), BF16),
            pltpu.VMEM((n_feat, own, latent), BF16),
            dma((5,)),
            dma((count // tile,)),
            dma((n_patch,)),
            dma((n_patch,)),
            dma((n_feat,)),
            dma((n_feat,)),
            dma((n_feat,)),
            dma((n_feat,)),
        ],
        compiler_params=pltpu.CompilerParams(
            collective_id=0, has_side_effects=True, vmem_limit_bytes=60 * 1024 * 1024
        ),
    )(
        live_edges,
        nodes,
        receivers.reshape(-1, LANES),
        sender_slot.reshape(-1, LANES),
        send_rows[0, 0],
        edge_b1.reshape(1, -1),
        edge_gain.reshape(1, -1),
        node_b1.reshape(1, -1),
        node_gain.reshape(1, -1),
        edges,
        edge_w1,
        edge_w2,
        node_w1,
        node_w2,
    )


def solution(mesh):
    both = P(("patch", "feat"))
    rows = P(("patch", "feat"), None)
    placed = (rows, rows, both, both, P("patch", "feat", None, None), both) + (P(),) * 8
    return jax.shard_map(
        functools.partial(local, mesh.shape["patch"], mesh.shape["feat"]),
        mesh=mesh,
        in_specs=placed,
        out_specs=(rows, rows),
        check_vma=False,
    )
```
